256 devices in a mesh: grp: 16 (over z, core), head: 16 (over y, x).
Axes of the slice: x: 4, y: 4, z: 8, core: 2. Of those that a mesh axis runs over, the one named last changes fastest.
Arguments:
- query_rows: bfloat16 [256, 128, 2048], P(('grp', 'head')), may hold values from -6 to 6
- key_rows: bfloat16 [256, 128, 2048], P(('grp', 'head')), may hold values from -6 to 6
- value_rows: bfloat16 [256, 128, 2048], P(('grp', 'head')), may hold values from -6 to 6
- log_decay: bfloat16 [256, 128, 2048], P(('grp', 'head')), may hold values from -1.5 to 0, as said below
- beta_logit: bfloat16 [256, 128, 16], P(('grp', 'head')), may hold values from -6 to 6
- out_grad: bfloat16 [256, 128, 2048], P(('grp', 'head')), may hold values from -6 to 6
- fork_state: float32 [8, 16, 128, 128], P(None, 'head'), may hold values from -6 to 6
- branch_prompt: int32 [256], replicated, may hold values from 0 to 7, as said below
- valid_len: int32 [256], replicated, may hold values from 32 to 128, as said below
Outputs:
- grad_query: bfloat16 [256, 128, 2048], P(('grp', 'head'))
- grad_key: bfloat16 [256, 128, 2048], P(('grp', 'head'))
- grad_value: bfloat16 [256, 128, 2048], P(('grp', 'head'))
- grad_decay: bfloat16 [256, 128, 2048], P(('grp', 'head'))
- grad_beta: bfloat16 [256, 128, 16], P(('grp', 'head'))
- grad_fork: float32 [8, 16, 128, 128], P(None, 'head')
The draws below stay inside these ranges and needn't reach their ends.
Inputs may be any that keep to these rules, and one draw needn't show every extreme that they name: `log_decay`: never positive; a few tokens of each branch lose a large share of every channel at once. `branch_prompt`: every prompt has at least one branch. A branch counts its first valid_len tokens; some branch uses all 128.
All inputs are finite; a program needn't handle non-finite values.
Results may differ from the reference program's by a relative error of at most 0.0015.
Values may be sent and summed in bfloat16 or wider, within the bound.
A program may use at most 64 MiB of HBM per device.

```python
import math
import jax
import jax.numpy as jnp
from jax import lax

HEADS = 16
HEAD_DIM = 128
WINDOW_TOKENS = 128
PROMPTS = 8
BRANCH_TOTAL = 256


def draw_log_decay(key, part):
    random_subkeys = jax.random.split(jax.random.fold_in(key, 11), 5)
    channels = HEADS * HEAD_DIM
    channel_decay_rate = jnp.exp(jax.random.uniform(random_subkeys[0], (channels,), jnp.float32, math.log(0.2 / WINDOW_TOKENS), math.log(0.04)))
    branch_factor = jnp.exp(jax.random.uniform(random_subkeys[1], (BRANCH_TOTAL, 1, 1), jnp.float32, math.log(0.5), math.log(2.0)))
    random_noise = jnp.exp(jax.random.uniform(random_subkeys[2], (BRANCH_TOTAL, WINDOW_TOKENS, channels), jnp.float32, math.log(0.5), math.log(2.0)))
    spike_position = jax.random.randint(random_subkeys[3], (BRANCH_TOTAL, 3), 0, WINDOW_TOKENS)
    spike_strength = jax.random.uniform(random_subkeys[4], (BRANCH_TOTAL, 3), jnp.float32, math.log(0.5), math.log(0.8))
    token_positions = jnp.arange(WINDOW_TOKENS, dtype=jnp.int32)
    spike_event = jnp.sum(jnp.where(token_positions[None, :, None] == spike_position[:, None, :], spike_strength[:, None, :], 0.0), axis=-1)
    output_values = -channel_decay_rate[None, None, :] * branch_factor * random_noise + spike_event[:, :, None]
    return output_values.astype(jnp.bfloat16)


def draw_branch_prompt(key, part):
    random_subkeys = jax.random.split(jax.random.fold_in(key, 23), 2)
    chosen = jax.random.randint(random_subkeys[0], (BRANCH_TOTAL,), 0, PROMPTS)
    spots = jax.random.permutation(random_subkeys[1], BRANCH_TOTAL)[:PROMPTS]
    return chosen.at[spots].set(jnp.arange(PROMPTS, dtype=jnp.int32)).astype(jnp.int32)


def draw_valid_len(key, part):
    random_subkeys = jax.random.split(jax.random.fold_in(key, 37), 2)
    lengths_out = jax.random.randint(random_subkeys[0], (BRANCH_TOTAL,), WINDOW_TOKENS // 4, WINDOW_TOKENS + 1)
    spot = jax.random.randint(random_subkeys[1], (), 0, BRANCH_TOTAL)
    return lengths_out.at[spot].set(WINDOW_TOKENS).astype(jnp.int32)


def level_of(rng, dims, shards, smallest, top_value):
    level = 1.0
    for axis_at, blocks in shards:
        heights = jax.random.uniform(jax.random.fold_in(jax.random.fold_in(rng, 6), axis_at), (blocks,), jnp.float32, smallest / len(shards), top_value / len(shards))
        level = level * jnp.repeat(jnp.exp(heights), dims[axis_at] // blocks).reshape((-1,) + (1,) * (len(dims) - 1 - axis_at))
    return level


def scatter_about(key, dims, scale, reach, cuts=(), kind=jnp.bfloat16):
    result = jax.random.normal(key, dims, jnp.float32) * scale
    if len(cuts) > 0:
        result = level_of(key, dims, cuts, -0.22, 0.18) * result
    return jnp.clip(result, min=-reach, max=reach).astype(kind)


def setup_inputs(seed: int = 0) -> dict:
    arg_keys = jax.random.split(jax.random.key(seed), 10)
    return {
        "query_rows": scatter_about(arg_keys[0], (BRANCH_TOTAL, WINDOW_TOKENS, HEADS * HEAD_DIM), 1.0, 6.0, ((0, 256),)),
        "key_rows": scatter_about(arg_keys[1], (BRANCH_TOTAL, WINDOW_TOKENS, HEADS * HEAD_DIM), 1.0, 6.0, ((0, 256),)),
        "value_rows": scatter_about(arg_keys[2], (BRANCH_TOTAL, WINDOW_TOKENS, HEADS * HEAD_DIM), 1.0, 6.0, ((0, 256),)),
        "log_decay": draw_log_decay(jax.random.fold_in(arg_keys[9], 71), 0),
        "beta_logit": scatter_about(arg_keys[4], (BRANCH_TOTAL, WINDOW_TOKENS, HEADS), 1.5, 6.0, ((0, 256),)),
        "out_grad": scatter_about(arg_keys[5], (BRANCH_TOTAL, WINDOW_TOKENS, HEADS * HEAD_DIM), 1.0, 6.0, ((0, 256),)),
        "fork_state": scatter_about(arg_keys[6], (PROMPTS, HEADS, HEAD_DIM, HEAD_DIM), 1.0, 6.0, ((1, 16),), jnp.float32),
        "branch_prompt": draw_branch_prompt(jax.random.fold_in(arg_keys[9], 71), 0),
        "valid_len": draw_valid_len(jax.random.fold_in(arg_keys[9], 71), 0),
    }


def decay_forward(query_in, key_in, value_in, decay_in, beta_in, state_in, keep_mask, block_len):
    head_dim = query_in.shape[-1]
    window_len = query_in.shape[1]
    upper_limit = lax.Precision.HIGHEST
    unit_query = query_in * lax.rsqrt(lax.optimization_barrier(jnp.sum(query_in * query_in, axis=-1, keepdims=True)) + 1e-06) * head_dim ** (-0.5)
    unit_key = key_in * lax.rsqrt(lax.optimization_barrier(jnp.sum(key_in * key_in, axis=-1, keepdims=True)) + 1e-06)
    beta_value = jax.nn.sigmoid(beta_in) * keep_mask[None, :]
    decay_value = decay_in * keep_mask[None, :, None]
    token_positions = jnp.arange(block_len, dtype=jnp.int32)
    lower_strict = (token_positions[:, None] > token_positions[None, :]).astype(jnp.float32)
    lower_closed = (token_positions[:, None] >= token_positions[None, :]).astype(jnp.float32)
    identity_block = jnp.eye(block_len, dtype=jnp.float32)
    outputs = []
    current_state = state_in
    for block_index in range(window_len // block_len):
        first_pos = block_index * block_len
        cum_decay = jnp.cumsum(decay_value[:, first_pos:first_pos + block_len], axis=1)
        growth = jnp.exp(cum_decay)
        shrink = jnp.exp(-cum_decay)
        key_block = unit_key[:, first_pos:first_pos + block_len]
        query_block = unit_query[:, first_pos:first_pos + block_len]
        block_value_rows = value_in[:, first_pos:first_pos + block_len]
        block_beta_rows = beta_value[:, first_pos:first_pos + block_len]
        key_forward_rows = key_block * growth
        key_earlier_rows = key_block * shrink
        query_forward_rows = query_block * growth
        coupling = jnp.einsum('htk,hsk->hts', key_forward_rows, key_earlier_rows, precision=upper_limit) * block_beta_rows[:, :, None] * lower_strict
        attend_scores = jnp.einsum('htk,hsk->hts', query_forward_rows, key_earlier_rows, precision=upper_limit) * lower_closed
        target_output = block_beta_rows[:, :, None] * (block_value_rows - jnp.einsum('led,ldf->lef', key_forward_rows, current_state, precision=upper_limit))
        state_update = jax.scipy.linalg.solve_triangular(identity_block + coupling, target_output, lower=True, unit_diagonal=True)
        output_block_rows = jnp.einsum('led,ldf->lef', query_forward_rows, current_state, precision=upper_limit) + jnp.einsum('ifj,ijo->ifo', attend_scores, state_update, precision=upper_limit)
        tail_increase = growth[:, -1, :]
        current_state = tail_increase[:, :, None] * current_state + jnp.einsum('lei,leg->lig', key_earlier_rows * tail_increase[:, None, :], state_update, precision=upper_limit)
        outputs.append(output_block_rows)
    return jnp.concatenate(outputs, axis=1)

def reference(query_rows, key_rows, value_rows, log_decay, beta_logit, out_grad, fork_state, branch_prompt, valid_len):
    block_len = min(64, WINDOW_TOKENS)

    def one_branch(fork_total, branch_index):

        def pick_branch(array_in):
            return lax.dynamic_index_in_dim(array_in, branch_index, 0, keepdims=False)

        def split_heads(array_in):
            return pick_branch(array_in).astype(jnp.float32).reshape(WINDOW_TOKENS, HEADS, HEAD_DIM).transpose(1, 0, 2)

        def join_heads(array_in):
            return array_in.transpose(1, 0, 2).reshape(WINDOW_TOKENS, HEADS * HEAD_DIM).astype(jnp.bfloat16)
        prompt_id = pick_branch(branch_prompt)
        keep_mask = (jnp.arange(WINDOW_TOKENS, dtype=jnp.int32) < pick_branch(valid_len)).astype(jnp.float32)
        state_in = lax.dynamic_index_in_dim(fork_state, prompt_id, 0, keepdims=False)
        beta_in = pick_branch(beta_logit).astype(jnp.float32).T

        def forward_one(query_in, key_in, value_in, decay_in, beta_one, state_one):
            return decay_forward(query_in, key_in, value_in, decay_in, beta_one, state_one, keep_mask, block_len)
        outputs, pullback = jax.vjp(forward_one, split_heads(query_rows), split_heads(key_rows), split_heads(value_rows), split_heads(log_decay), beta_in, state_in)
        cotangent = split_heads(out_grad) * keep_mask[None, :, None]
        grad_q, grad_k, grad_v, grad_g, grad_b, grad_s = pullback(cotangent)
        previous = lax.dynamic_index_in_dim(fork_total, prompt_id, 0, keepdims=False)
        fork_total = lax.dynamic_update_index_in_dim(fork_total, previous + grad_s, prompt_id, 0)
        return (fork_total, (join_heads(grad_q), join_heads(grad_k), join_heads(grad_v), join_heads(grad_g), grad_b.T.astype(jnp.bfloat16)))
    start_total = jnp.zeros((PROMPTS, HEADS, HEAD_DIM, HEAD_DIM), jnp.float32)
    fork_total, per_branch = lax.scan(one_branch, start_total, jnp.arange(BRANCH_TOTAL, dtype=jnp.int32))
    return (per_branch[0], per_branch[1], per_branch[2], per_branch[3], per_branch[4], fork_total)
```

```python
import jax
import jax.numpy as jnp
from jax import lax
from jax.experimental import pallas as pl
from jax.experimental.pallas import tpu as pltpu
from jax.sharding import PartitionSpec as P

F32 = jnp.float32
BF16 = jnp.bfloat16
MESH = pl.DeviceIdType.MESH
D = 128
HALF = 64
HEADS = 16
GROUPS = 16
PROMPTS = 8
HA = 2
HB = 2
SCALE = D**-0.5


def dot(a, b, ca, cb):
    return lax.dot_general(a, b, (((ca,), (cb,)), ((), ())), preferred_element_type=F32)


def split(x):
    hi = x.astype(BF16)
    return hi, (x - hi.astype(F32)).astype(BF16)


def cat(parts, axis):
    return jnp.concatenate(parts, axis=axis)


def mm3(a, b, ca, cb):
    return dot(cat([a[0], a[0], a[1]], ca), cat([b[0], b[1], b[0]], cb), ca, cb)


def mm2(a, b, ca, cb):
    return dot(cat([a, a], ca), cat([b[0], b[1]], cb), ca, cb)


def kernel(
    prompt_ref, len_ref, q_ref, k_ref, v_ref, g_ref, beta_ref, do_ref, fork_ref,
    gq_ref, gk_ref, gv_ref, gg_ref, gb_ref, gf_ref,
    s_send, s_recv, ds_send, ds_recv, acc, pair_recv, comb, rs_recv,
    u_s, w_s, decay_s, qf_s, kf_s, ke_s, kt_s, tt_s, mask_s, tri_s, beta_s, betat_s, gb_s,
    s_ssem, s_rsem, d_ssem, d_rsem, p_ssem, p_rsem, r_ssem, r_rsem, a_ssem, a_rsem, f_ssem, f_rsem,
):
    grp = lax.axis_index("grp")
    me = lax.axis_index("head")
    core = lax.rem(grp, 2)
    zed = grp // 2
    base = grp * HEADS

    def head_peer(o):
        return (grp, lax.rem(me + o, HEADS))

    def z_peer(o):
        return (lax.rem(zed + o, PROMPTS) * 2 + core, me)

    partner = (zed * 2 + 1 - core, me)

    barrier = pltpu.get_barrier_semaphore()

    def greet_head(o, c):
        pl.semaphore_signal(barrier, inc=1, device_id=head_peer(o), device_id_type=MESH)
        return c

    def greet_z(o, c):
        pl.semaphore_signal(barrier, inc=1, device_id=z_peer(o), device_id_type=MESH)
        return c

    lax.fori_loop(1, HEADS, greet_head, 0)
    lax.fori_loop(1, PROMPTS, greet_z, 0)
    pl.semaphore_signal(barrier, inc=1, device_id=partner, device_id_type=MESH)

    def pack_state(o, c):
        s_send[o] = fork_ref[prompt_ref[base + lax.rem(me + o, HEADS)], 0]
        return c

    s_recv[0] = fork_ref[prompt_ref[base + me], 0]
    lax.fori_loop(1, HEADS, pack_state, 0)

    row = lax.broadcasted_iota(jnp.int32, (D, D), 0)
    col = lax.broadcasted_iota(jnp.int32, (D, D), 1)
    xor = jnp.where(row < col, jnp.bitwise_xor(row, col), 0)
    for level in range(7):
        m = 1 << level
        mask_s[level] = jnp.where((xor >= m) & (xor < 2 * m), 1.0, 0.0).astype(BF16)
    lower = jnp.where(col <= row, 1.0, 0.0) - jnp.where(col < HALF, 1.0, 0.0)
    tri_s[0] = lower.astype(BF16)
    tri_s[1] = jnp.where(col >= row, 1.0, 0.0).astype(BF16)
    valid = len_ref[base + me]
    keep_col = jnp.where(lax.broadcasted_iota(jnp.int32, (D, 1), 0) < valid, 1.0, 0.0)
    beta_all = jax.nn.sigmoid(beta_ref[0].astype(F32))
    beta_pad = cat([beta_all, jnp.zeros((D, D - HEADS), F32)], 1) * keep_col
    beta_s[...] = beta_pad
    betat_s[...] = beta_pad.T
    gb_s[...] = jnp.zeros((D, D), F32)

    pl.semaphore_wait(barrier, HEADS - 1 + PROMPTS - 1 + 1)

    def state_copy(o):
        return pltpu.make_async_remote_copy(
            src_ref=s_send.at[o], dst_ref=s_recv.at[o], send_sem=s_ssem.at[o], recv_sem=s_rsem.at[o],
            device_id=head_peer(o), device_id_type=MESH)

    def send_state(o, c):
        state_copy(o).start()
        return c

    lax.fori_loop(1, HEADS, send_state, 0)

    def head_lanes(h):
        return pl.ds(pl.multiple_of(h * D, D), D)

    def beta_column(h):
        return jnp.sum(jnp.where(col == h, beta_s[...], 0.0), axis=1, keepdims=True)

    def keep_rows():
        return lax.broadcasted_iota(jnp.int32, (D, 1), 0) < valid

    def slot_of(h):
        return lax.rem(h - me + HEADS, HEADS)

    def grad_copy(h):
        o = slot_of(h)
        return pltpu.make_async_remote_copy(
            src_ref=ds_send.at[o], dst_ref=ds_recv.at[o], send_sem=d_ssem.at[o], recv_sem=d_rsem.at[o],
            device_id=(grp, h), device_id_type=MESH)

    def phase_a(h):
        lanes = head_lanes(h)
        keep = keep_rows()
        q = q_ref[0, :, lanes].astype(F32)
        k = k_ref[0, :, lanes].astype(F32)
        uq = q * (lax.rsqrt(jnp.sum(q * q, axis=1, keepdims=True) + 1e-6) * SCALE)
        uk = k * lax.rsqrt(jnp.sum(k * k, axis=1, keepdims=True) + 1e-6)
        decay = jnp.where(keep, g_ref[0, :, lanes].astype(F32), 0.0)
        cum = dot(tri_s[0], decay.astype(BF16), 1, 0)
        ee = jnp.exp(decay[0:1] - cum[0:1])
        eg = jnp.exp(cum)
        es = jnp.exp(-cum)
        qf, kf = uq * eg, uk * eg
        qfs, kfs, kes = split(qf), split(kf), split(uk * es)
        qts, kts = split(qf * ee), split(kf * ee)
        u_s[h, 0], u_s[h, 1] = uq, uk
        decay_s[h, 0], decay_s[h, 1] = eg, es
        for i in range(2):
            qf_s[h, i], kf_s[h, i], ke_s[h, i], kt_s[h, i] = qfs[i], kfs[i], kes[i], kts[i]
        both = tuple(cat([kfs[i], qfs[i]], 0) for i in range(2))
        scores = mm3(kes, both, 1, 1)
        beta_row = betat_s[pl.ds(h, 1), :]
        coupling = split(jnp.where(row < col, scores[:, :D] * beta_row, 0.0))
        attend = split(jnp.where(row <= col, scores[:, D:], 0.0))
        do = jnp.where(keep, do_ref[0, :, lanes].astype(F32), 0.0).astype(BF16)
        du = split(dot(cat([attend[0], attend[1]], 1), cat([do, do], 0), 1, 0))
        eye = jnp.where(row == col, 1.0, 0.0)
        inv = eye - (coupling[0] * mask_s[0]).astype(F32) - (coupling[1] * mask_s[0]).astype(F32)
        for level in range(1, 7):
            mask = mask_s[level]
            inv_p = split(inv)
            step = split(mm3((coupling[0] * mask, coupling[1] * mask), inv_p, 1, 0))
            inv = inv - mm3(inv_p, step, 1, 0)
        inv_p = split(inv)
        tt_s[h, 0], tt_s[h, 1] = inv_p
        w = mm3(inv_p, du, 1, 0)
        w_s[h] = w
        nbw = split(-(beta_column(h) * w))
        ds = dot(
            cat([qts[0], qts[1], kts[0], kts[0], kts[1]], 0),
            cat([do, do, nbw[0], nbw[1], nbw[0]], 0), 0, 0)
        o = slot_of(h)
        ds_send[o] = ds

        @pl.when(o == 0)
        def _():
            ds_recv[0] = ds

    def phase_b(h):
        lanes = head_lanes(h)
        keep = keep_rows()
        q = q_ref[0, :, lanes].astype(F32)
        k = k_ref[0, :, lanes].astype(F32)
        rq = lax.rsqrt(jnp.sum(q * q, axis=1, keepdims=True) + 1e-6)
        rk = lax.rsqrt(jnp.sum(k * k, axis=1, keepdims=True) + 1e-6)
        uq, uk = u_s[h, 0], u_s[h, 1]
        eg, es = decay_s[h, 0], decay_s[h, 1]
        pair = lambda ref: (ref[h, 0], ref[h, 1])
        qfs, kfs, kes, kts, tts = pair(qf_s), pair(kf_s), pair(ke_s), pair(kt_s), pair(tt_s)
        w = w_s[h]
        beta = beta_column(h)
        nbw_f = -(beta * w)
        nbw = split(nbw_f)
        do = jnp.where(keep, do_ref[0, :, lanes].astype(F32), 0.0).astype(BF16)
        ss = split(s_recv[lax.rem(me - h + HEADS, HEADS)])
        v = v_ref[0, :, lanes].astype(F32)
        target = split(beta * (v - mm3(kts, ss, 1, 0)))
        u = mm3(tts, target, 0, 0)
        us = split(u)
        dp = split(jnp.where(row >= col, mm2(do, us, 1, 1), 0.0))
        dn = split(jnp.where(row > col, mm3(nbw, us, 1, 1), 0.0))
        decay0 = jnp.where(keep, g_ref[0, :, lanes].astype(F32), 0.0)[0:1]
        cum0 = dot(tri_s[0, 0:16], jnp.where(keep, g_ref[0, :, lanes].astype(F32), 0.0).astype(BF16), 1, 0)[0:1]
        ee = jnp.exp(decay0 - cum0)
        dqf = mm2(do, ss, 1, 1) * ee + mm3(dp, kes, 1, 0)
        dkf = mm3(nbw, ss, 1, 1) * ee + mm3(dn, kes, 1, 0)
        dke = dot(
            cat([dn[0], dn[0], dn[1], dp[0], dp[0], dp[1]], 0),
            cat([kfs[0], kfs[1], kfs[0], qfs[0], qfs[1], qfs[0]], 0), 0, 0)
        dqg, dkg, dks = dqf * eg, dkf * eg, dke * es
        dc = split(dqg * uq + dkg * uk - dks * uk)
        dg = mm2(tri_s[1], dc, 1, 0)
        gg_ref[0, :, lanes] = jnp.where(keep, dg, 0.0).astype(BF16)
        duk = dkg + dks
        gq = rq * (SCALE * dqg - uq * (jnp.sum(uq * dqg, axis=1, keepdims=True) * (1.0 / SCALE)))
        gk = rk * (duk - uk * jnp.sum(uk * duk, axis=1, keepdims=True))
        gq_ref[0, :, lanes] = gq.astype(BF16)
        gk_ref[0, :, lanes] = gk.astype(BF16)
        gv_ref[0, :, lanes] = (-nbw_f).astype(BF16)
        db = jnp.where(keep, (1.0 - beta) * jnp.sum(w * u, axis=1, keepdims=True), 0.0)
        gb_s[...] = jnp.where(col == h, db, gb_s[...])

    def loop_a(i, c):
        first = lax.rem(me // HA + i, HEADS // HA) * HA
        for n in range(HA):
            phase_a(first + n)
        for n in range(HA):
            h = first + n

            @pl.when(h != me)
            def _():
                grad_copy(h).start()

        return c

    lax.fori_loop(0, HEADS // HA, loop_a, 0)

    def wait_state(o, c):
        state_copy(o).wait()
        return c

    lax.fori_loop(1, HEADS, wait_state, 0)

    def pair_copy():
        return pltpu.make_async_remote_copy(
            src_ref=acc.at[1 - core], dst_ref=pair_recv, send_sem=p_ssem, recv_sem=p_rsem,
            device_id=partner, device_id_type=MESH)

    def rs_copy(o):
        return pltpu.make_async_remote_copy(
            src_ref=comb.at[lax.rem(zed + o, PROMPTS)], dst_ref=rs_recv.at[o],
            send_sem=r_ssem.at[o], recv_sem=r_rsem.at[o], device_id=z_peer(o), device_id_type=MESH)

    def piece(p, c):
        return gf_ref.at[p, 0, pl.ds(pl.multiple_of(c * HALF, HALF), HALF)]

    def ag_copy(o):
        return pltpu.make_async_remote_copy(
            src_ref=piece(zed, core), dst_ref=piece(zed, core),
            send_sem=a_ssem.at[o], recv_sem=a_rsem.at[o], device_id=z_peer(o), device_id_type=MESH)

    def hand_copy(o):
        p = lax.rem(zed - o + PROMPTS, PROMPTS)
        return pltpu.make_async_remote_copy(
            src_ref=piece(p, core), dst_ref=piece(p, core),
            send_sem=f_ssem.at[o], recv_sem=f_rsem.at[o], device_id=partner, device_id_type=MESH)

    def stage_sum():
        def wait_grad(o, c):
            copy = pltpu.make_async_remote_copy(
                src_ref=ds_send.at[o], dst_ref=ds_recv.at[o], send_sem=d_ssem.at[o], recv_sem=d_rsem.at[o],
                device_id=head_peer(o), device_id_type=MESH)
            copy.wait()
            return c

        lax.fori_loop(1, HEADS, wait_grad, 0)

        def sum_rows(r, c):
            half = r // 8
            rows = pl.ds(pl.multiple_of(r * 8, 8), 8)
            out_rows = pl.ds(pl.multiple_of(lax.rem(r, 8) * 8, 8), 8)
            totals = [jnp.zeros((8, D), F32)] * PROMPTS
            for o in range(HEADS):
                part = ds_recv[o, rows, :]
                source = prompt_ref[base + lax.rem(me - o + HEADS, HEADS)]
                for p in range(PROMPTS):
                    totals[p] = totals[p] + jnp.where(source == p, 1.0, 0.0) * part
            for p in range(PROMPTS):
                acc[half, p, out_rows, :] = totals[p]
            return c

        lax.fori_loop(0, 16, sum_rows, 0)
        pair_copy().start()

    def stage_scatter():
        pair_copy().wait()
        comb[...] = acc[core] + pair_recv[...]
        lax.fori_loop(1, PROMPTS, lambda o, c: (rs_copy(o).start(), c)[1], 0)

    def stage_gather():
        lax.fori_loop(1, PROMPTS, lambda o, c: (rs_copy(o).wait(), c)[1], 0)
        total = comb[zed]
        for o in range(1, PROMPTS):
            total = total + rs_recv[o]
        gf_ref[zed, 0, pl.ds(pl.multiple_of(core * HALF, HALF), HALF)] = total
        lax.fori_loop(1, PROMPTS, lambda o, c: (ag_copy(o).start(), c)[1], 0)
        hand_copy(0).start()

    def stage_hand():
        def forward(o, c):
            ag_copy(o).wait()
            hand_copy(o).start()
            return c

        lax.fori_loop(1, PROMPTS, forward, 0)

    steps = HEADS // HB
    stages = {1: stage_sum, 2: stage_scatter, 4: stage_gather, 6: stage_hand}

    def loop_b(i, c):
        for at, stage in stages.items():
            pl.when(i == at)(stage)
        for n in range(HB):
            phase_b(i * HB + n)
        return c

    lax.fori_loop(0, steps, loop_b, 0)
    gb_ref[0] = gb_s[:, :HEADS].astype(BF16)
    lax.fori_loop(0, PROMPTS, lambda o, c: (hand_copy(o).wait(), c)[1], 0)


def per_device(query_rows, key_rows, value_rows, log_decay, beta_logit, out_grad, fork_state, branch_prompt, valid_len):
    vmem = pl.BlockSpec(memory_space=pltpu.VMEM)
    smem = pl.BlockSpec(memory_space=pltpu.SMEM)
    rows = jax.ShapeDtypeStruct(query_rows.shape, BF16)
    dma = pltpu.SemaphoreType.DMA
    pairs = pltpu.VMEM((HEADS, 2, D, D), BF16)
    return pl.pallas_call(
        kernel,
        out_shape=(
            rows, rows, rows, rows,
            jax.ShapeDtypeStruct(beta_logit.shape, BF16),
            jax.ShapeDtypeStruct(fork_state.shape, F32),
        ),
        in_specs=[smem, smem] + [vmem] * 7,
        out_specs=(vmem,) * 6,
        scratch_shapes=[
            pltpu.VMEM((HEADS, D, D), F32),
            pltpu.VMEM((HEADS, D, D), F32),
            pltpu.VMEM((HEADS, D, D), F32),
            pltpu.VMEM((HEADS, D, D), F32),
            pltpu.VMEM((2, PROMPTS, HALF, D), F32),
            pltpu.VMEM((PROMPTS, HALF, D), F32),
            pltpu.VMEM((PROMPTS, HALF, D), F32),
            pltpu.VMEM((PROMPTS, HALF, D), F32),
            pltpu.VMEM((HEADS, 2, D, D), F32),
            pltpu.VMEM((HEADS, D, D), F32),
            pltpu.VMEM((HEADS, 2, D, D), F32),
            pairs, pairs, pairs, pairs, pairs,
            pltpu.VMEM((7, D, D), BF16),
            pltpu.VMEM((2, D, D), BF16),
            pltpu.VMEM((D, D), F32),
            pltpu.VMEM((D, D), F32),
            pltpu.VMEM((D, D), F32),
            dma((HEADS,)), dma((HEADS,)),
            dma((HEADS,)), dma((HEADS,)),
            dma(()), dma(()),
            dma((PROMPTS,)), dma((PROMPTS,)),
            dma((PROMPTS,)), dma((PROMPTS,)),
            dma((PROMPTS,)), dma((PROMPTS,)),
        ],
        compiler_params=pltpu.CompilerParams(collective_id=0, has_side_effects=True),
        name="delta_backward",
    )(branch_prompt, valid_len, query_rows, key_rows, value_rows, log_decay, beta_logit, out_grad, fork_state)


def solution(mesh):
    branch = P(("grp", "head"), None, None)
    state = P(None, "head", None, None)
    return jax.shard_map(
        per_device,
        mesh=mesh,
        in_specs=(branch,) * 6 + (state, P(), P()),
        out_specs=(branch,) * 5 + (state,),
        check_vma=False,
    )
```

```python
import jax
import jax.numpy as jnp
from jax import lax
from jax.experimental import pallas as pl
from jax.experimental.pallas import tpu as pltpu
from jax.sharding import PartitionSpec as P

F32 = jnp.float32
BF16 = jnp.bfloat16
I16 = jnp.int16
MESH = pl.DeviceIdType.MESH
D = 128
HALF = 64
HEADS = 16
GROUPS = 16
PROMPTS = 8
HA = 8
HB = 4
TAIL = 16
STAGE_SUM = 2
STAGE_SCATTER = 3
STAGE_GATHER = 4
STAGE_HAND = 4
SCALE = D**-0.5


def dot(a, b, ca, cb):
    return lax.dot_general(a, b, (((ca,), (cb,)), ((), ())), preferred_element_type=F32)


def split(x):
    hi = x.astype(BF16)
    return hi, (x - hi.astype(F32)).astype(BF16)


def cat(parts, axis):
    return jnp.concatenate(parts, axis=axis)


def mm3(a, b, ca, cb):
    return dot(cat([a[0], a[0], a[1]], ca), cat([b[0], b[1], b[0]], cb), ca, cb)


def mm2(a, b, ca, cb):
    return dot(cat([a, a], ca), cat([b[0], b[1]], cb), ca, cb)


def encode(x):
    peak = jnp.maximum(jnp.max(jnp.abs(x), axis=0, keepdims=True), 1e-30)
    power = jnp.ceil(jnp.log2(peak))
    code = jnp.clip(jnp.round(x * jnp.exp2(15.0 - power)), -32767.0, 32767.0)
    tail = jnp.broadcast_to(power, (TAIL, x.shape[1]))
    return cat([code, tail], 0).astype(jnp.int32).astype(I16)


def decode(code, tail):
    power = tail[0:1].astype(jnp.int32).astype(F32)
    return code.astype(jnp.int32).astype(F32) * jnp.exp2(power - 15.0)


def kernel(
    prompt_ref, len_ref, q_ref, k_ref, v_ref, g_ref, beta_ref, do_ref, fork_ref,
    gq_ref, gk_ref, gv_ref, gg_ref, gb_ref, gf_ref,
    s_own, s_send, s_recv, ds_send, ds_recv, acc, pair_recv, comb, rs_send, rs_recv, ag,
    u_s, w_s, decay_s, ee_s, qf_s, kf_s, ke_s, kt_s, tt_s, mask_s, tri_s, beta_s, betat_s, gb_s,
    s_ssem, s_rsem, d_ssem, d_rsem, p_ssem, p_rsem, r_ssem, r_rsem, a_ssem, a_rsem, f_ssem, f_rsem,
):
    grp = lax.axis_index("grp")
    me = lax.axis_index("head")
    core = lax.rem(grp, 2)
    zed = grp // 2
    base = grp * HEADS

    def head_peer(o):
        return (grp, lax.rem(me + o, HEADS))

    def z_peer(o):
        return (lax.rem(zed + o, PROMPTS) * 2 + core, me)

    partner = (zed * 2 + 1 - core, me)

    barrier = pltpu.get_barrier_semaphore()

    def greet_head(o, c):
        pl.semaphore_signal(barrier, inc=1, device_id=head_peer(o), device_id_type=MESH)
        return c

    def greet_z(o, c):
        pl.semaphore_signal(barrier, inc=1, device_id=z_peer(o), device_id_type=MESH)
        return c

    lax.fori_loop(1, HEADS, greet_head, 0)
    lax.fori_loop(1, PROMPTS, greet_z, 0)
    pl.semaphore_signal(barrier, inc=1, device_id=partner, device_id_type=MESH)

    def pack_state(o, c):
        s_send[o] = encode(fork_ref[prompt_ref[base + lax.rem(me + o, HEADS)], 0])
        return c

    s_recv[0] = encode(fork_ref[prompt_ref[base + me], 0])
    s_own[...] = fork_ref[prompt_ref[base + me], 0]
    lax.fori_loop(1, HEADS, pack_state, 0)

    row = lax.broadcasted_iota(jnp.int32, (D, D), 0)
    col = lax.broadcasted_iota(jnp.int32, (D, D), 1)
    xor = jnp.where(row < col, jnp.bitwise_xor(row, col), 0)
    for level in range(7):
        m = 1 << level
        mask_s[level] = jnp.where((xor >= m) & (xor < 2 * m), 1.0, 0.0).astype(BF16)
    lower = jnp.where(col <= row, 1.0, 0.0) - jnp.where(col < HALF, 1.0, 0.0)
    tri_s[0] = lower.astype(BF16)
    tri_s[1] = jnp.where(col >= row, 1.0, 0.0).astype(BF16)
    valid = len_ref[base + me]
    keep_lane = jnp.where(lax.broadcasted_iota(jnp.int32, (1, D), 1) < valid, 1.0, 0.0)
    beta_rows = jax.nn.sigmoid(beta_ref[0].astype(F32)) * keep_lane
    beta_pad = cat([beta_rows, jnp.zeros((D - HEADS, D), F32)], 0)
    betat_s[...] = beta_pad
    beta_s[...] = beta_pad.T
    gb_s[...] = jnp.zeros((D, D), F32)

    pl.semaphore_wait(barrier, HEADS - 1 + PROMPTS - 1 + 1)

    def state_copy(o):
        return pltpu.make_async_remote_copy(
            src_ref=s_send.at[o], dst_ref=s_recv.at[o], send_sem=s_ssem.at[o], recv_sem=s_rsem.at[o],
            device_id=head_peer(o), device_id_type=MESH)

    def send_state(o, c):
        state_copy(o).start()
        return c

    lax.fori_loop(1, HEADS, send_state, 0)

    def head_lanes(h):
        return pl.ds(pl.multiple_of(h * D, D), D)

    def beta_column(h):
        return jnp.sum(jnp.where(col == h, beta_s[...], 0.0), axis=1, keepdims=True)

    def keep_rows():
        return lax.broadcasted_iota(jnp.int32, (D, 1), 0) < valid

    def slot_of(h):
        return lax.rem(h - me + HEADS, HEADS)

    def grad_copy(h):
        o = slot_of(h)
        return pltpu.make_async_remote_copy(
            src_ref=ds_send.at[o], dst_ref=ds_recv.at[o], send_sem=d_ssem.at[o], recv_sem=d_rsem.at[o],
            device_id=(grp, h), device_id_type=MESH)

    def unit_parts(h):
        lanes = head_lanes(h)
        q = q_ref[0, :, lanes].astype(F32)
        k = k_ref[0, :, lanes].astype(F32)
        rq = lax.rsqrt(jnp.sum(q * q, axis=1, keepdims=True) + 1e-6)
        rk = lax.rsqrt(jnp.sum(k * k, axis=1, keepdims=True) + 1e-6)
        return q, k, rq, rk

    def masked_grad(h):
        return jnp.where(keep_rows(), do_ref[0, :, head_lanes(h)].astype(F32), 0.0).astype(BF16)

    def decay_rows(h):
        return jnp.where(keep_rows(), g_ref[0, :, head_lanes(h)].astype(F32), 0.0)

    def prepare(h):
        q, k, rq, rk = unit_parts(h)
        uq, uk = q * (rq * SCALE), k * rk
        decay = decay_rows(h)
        cum = dot(tri_s[0], decay.astype(BF16), 1, 0)
        ee = jnp.exp(decay[0:1] - cum[0:1])
        eg = jnp.exp(cum)
        es = jnp.exp(-cum)
        qf, kf = uq * eg, uk * eg
        qfs, kfs, kes = split(qf), split(kf), split(uk * es)
        qts, kts = split(qf * ee), split(kf * ee)
        u_s[h, 0], u_s[h, 1] = uq, uk
        decay_s[h, 0], decay_s[h, 1] = eg, es
        ee_s[h] = jnp.broadcast_to(ee, (8, D))
        for i in range(2):
            qf_s[h, i], kf_s[h, i], ke_s[h, i], kt_s[h, i] = qfs[i], kfs[i], kes[i], kts[i]
        return qfs, kfs, kes, qts, kts

    def couple(h, qfs, kfs, kes):
        both = tuple(cat([kfs[i], qfs[i]], 0) for i in range(2))
        scores = mm3(kes, both, 1, 1)
        beta_row = betat_s[pl.ds(h, 1), :]
        coupling = split(jnp.where(row < col, scores[:, :D] * beta_row, 0.0))
        attend = split(jnp.where(row <= col, scores[:, D:], 0.0))
        return coupling, attend

    def phase_a(hs):
        prep = [prepare(h) for h in hs]
        scores = [couple(h, *p[:3]) for h, p in zip(hs, prep)]
        dos = [masked_grad(h) for h in hs]
        dus = [split(dot(cat([a[0], a[1]], 1), cat([do, do], 0), 1, 0)) for (_, a), do in zip(scores, dos)]
        eye = jnp.where(row == col, 1.0, 0.0)
        invs = [eye - (c[0] * mask_s[0]).astype(F32) - (c[1] * mask_s[0]).astype(F32) for c, _ in scores]
        for level in range(1, 7):
            mask = mask_s[level]
            inv_ps = [split(x) for x in invs]
            steps_f = [mm3((c[0] * mask, c[1] * mask), ip, 1, 0) for (c, _), ip in zip(scores, inv_ps)]
            steps_p = [split(x) for x in steps_f]
            invs = [x - mm3(ip, sp, 1, 0) for x, ip, sp in zip(invs, inv_ps, steps_p)]
        inv_ps = [split(x) for x in invs]
        for h, ip in zip(hs, inv_ps):
            tt_s[h, 0], tt_s[h, 1] = ip
        ws = [mm3(ip, du, 1, 0) for ip, du in zip(inv_ps, dus)]
        nbws = []
        for h, w in zip(hs, ws):
            w_s[h] = w
            nbws.append(split(-(beta_column(h) * w)))
        dss = [
            dot(
                cat([p[3][0], p[3][1], p[4][0], p[4][0], p[4][1]], 0),
                cat([do, do, nbw[0], nbw[1], nbw[0]], 0), 0, 0)
            for p, do, nbw in zip(prep, dos, nbws)]
        for h, ds in zip(hs, dss):
            ds_send[slot_of(h)] = encode(ds)

    def phase_b(hs):
        pair = lambda ref: [(ref[h, 0], ref[h, 1]) for h in hs]
        betas = [beta_column(h) for h in hs]
        kts, tts = pair(kt_s), pair(tt_s)
        sss = []
        for h in hs:
            o = lax.rem(me - h + HEADS, HEADS)
            state = decode(s_recv[o, 0:D], s_recv[o, D : D + TAIL])
            sss.append(split(jnp.where(o == 0, s_own[...], state)))
        reads = [mm3(kt, ss, 1, 0) for kt, ss in zip(kts, sss)]
        targets = [
            split(b * (v_ref[0, :, head_lanes(h)].astype(F32) - r))
            for h, b, r in zip(hs, betas, reads)]
        us = [mm3(tt, tg, 0, 0) for tt, tg in zip(tts, targets)]
        usp = [split(u) for u in us]
        dos = [masked_grad(h) for h in hs]
        nbw_fs = [-(b * w_s[h]) for h, b in zip(hs, betas)]
        nbws = [split(x) for x in nbw_fs]
        dps = [split(jnp.where(row >= col, mm2(do, u, 1, 1), 0.0)) for do, u in zip(dos, usp)]
        dns = [split(jnp.where(row > col, mm3(nbw, u, 1, 1), 0.0)) for nbw, u in zip(nbws, usp)]
        kes, kfs, qfs = pair(ke_s), pair(kf_s), pair(qf_s)
        ees = [ee_s[h][0:1] for h in hs]
        dqfs = [mm2(do, ss, 1, 1) * ee + mm3(dp, ke, 1, 0) for do, ss, ee, dp, ke in zip(dos, sss, ees, dps, kes)]
        dkfs = [mm3(nbw, ss, 1, 1) * ee + mm3(dn, ke, 1, 0) for nbw, ss, ee, dn, ke in zip(nbws, sss, ees, dns, kes)]
        dkes = [
            dot(
                cat([dn[0], dn[0], dn[1], dp[0], dp[0], dp[1]], 0),
                cat([kf[0], kf[1], kf[0], qf[0], qf[1], qf[0]], 0), 0, 0)
            for dn, dp, kf, qf in zip(dns, dps, kfs, qfs)]
        for n, h in enumerate(hs):
            lanes = head_lanes(h)
            keep = keep_rows()
            uq, uk = u_s[h, 0], u_s[h, 1]
            eg, es = decay_s[h, 0], decay_s[h, 1]
            dqg, dkg, dks = dqfs[n] * eg, dkfs[n] * eg, dkes[n] * es
            dc = split(dqg * uq + dkg * uk - dks * uk)
            dg = mm2(tri_s[1], dc, 1, 0)
            gg_ref[0, :, lanes] = jnp.where(keep, dg, 0.0).astype(BF16)
            _, _, rq, rk = unit_parts(h)
            duk = dkg + dks
            gq = rq * (SCALE * dqg - uq * (jnp.sum(uq * dqg, axis=1, keepdims=True) * (1.0 / SCALE)))
            gk = rk * (duk - uk * jnp.sum(uk * duk, axis=1, keepdims=True))
            gq_ref[0, :, lanes] = gq.astype(BF16)
            gk_ref[0, :, lanes] = gk.astype(BF16)
            gv_ref[0, :, lanes] = (-nbw_fs[n]).astype(BF16)
            db = jnp.where(keep, (1.0 - betas[n]) * jnp.sum(w_s[h] * us[n], axis=1, keepdims=True), 0.0)
            gb_s[...] = jnp.where(col == h, db, gb_s[...])

    def loop_a(i, c):
        first = lax.rem(me // HA + i, HEADS // HA) * HA
        phase_a([first + n for n in range(HA)])
        for n in range(HA):
            h = first + n

            @pl.when(h != me)
            def _():
                grad_copy(h).start()

        return c

    lax.fori_loop(0, HEADS // HA, loop_a, 0)

    def wait_state(o, c):
        state_copy(o).wait()
        return c

    lax.fori_loop(1, HEADS, wait_state, 0)

    def pair_copy():
        return pltpu.make_async_remote_copy(
            src_ref=acc.at[1 - core], dst_ref=pair_recv, send_sem=p_ssem, recv_sem=p_rsem,
            device_id=partner, device_id_type=MESH)

    def rs_copy(o):
        return pltpu.make_async_remote_copy(
            src_ref=rs_send.at[lax.rem(zed + o, PROMPTS)], dst_ref=rs_recv.at[o],
            send_sem=r_ssem.at[o], recv_sem=r_rsem.at[o], device_id=z_peer(o), device_id_type=MESH)

    def piece(p, c):
        return ag.at[c, p]

    def ag_copy(o):
        return pltpu.make_async_remote_copy(
            src_ref=piece(zed, core), dst_ref=piece(zed, core),
            send_sem=a_ssem.at[o], recv_sem=a_rsem.at[o], device_id=z_peer(o), device_id_type=MESH)

    def hand_copy(o):
        p = lax.rem(zed - o + PROMPTS, PROMPTS)
        return pltpu.make_async_remote_copy(
            src_ref=piece(p, core), dst_ref=piece(p, core),
            send_sem=f_ssem.at[o], recv_sem=f_rsem.at[o], device_id=partner, device_id_type=MESH)

    def stage_sum():
        def wait_grad(o, c):
            copy = pltpu.make_async_remote_copy(
                src_ref=ds_send.at[o], dst_ref=ds_recv.at[o], send_sem=d_ssem.at[o], recv_sem=d_rsem.at[o],
                device_id=head_peer(o), device_id_type=MESH)
            copy.wait()
            return c

        lax.fori_loop(1, HEADS, wait_grad, 0)

        ds_recv[0] = ds_send[0]
        r64 = lax.broadcasted_iota(jnp.int32, (HALF, D), 0)
        c64 = lax.broadcasted_iota(jnp.int32, (HALF, D), 1)
        source = jnp.zeros((HALF, D), jnp.int32)
        for o in range(HEADS):
            source = jnp.where(c64 // 8 == o, prompt_ref[base + lax.rem(me - o + HEADS, HEADS)], source)
        hit = (source == r64 // 8) & (lax.rem(c64, 8) == lax.rem(r64, 8))
        pick = jnp.where(hit, 1.0, 0.0).astype(BF16)
        pick = cat([pick, pick], 1)

        def sum_rows(r, c):
            half = r // 4
            rows = pl.ds(pl.multiple_of(r * 16, 16), 16)
            parts = [decode(ds_recv[o, rows, :], ds_recv[o, D : D + TAIL, :]) for o in range(HEADS)]
            for n in range(2):
                stack = split(cat([p[8 * n : 8 * n + 8] for p in parts], 0))
                total = dot(pick, cat(stack, 0), 1, 0)
                out_rows = pl.ds(pl.multiple_of(lax.rem(r, 4) * 16 + 8 * n, 8), 8)
                for p in range(PROMPTS):
                    acc[half, p, out_rows, :] = total[8 * p : 8 * p + 8]
            return c

        lax.fori_loop(0, 8, sum_rows, 0)
        pair_copy().start()

    def stage_scatter():
        pair_copy().wait()
        for p in range(PROMPTS):
            both = acc[core, p] + pair_recv[p]
            comb[p] = both
            rs_send[p] = encode(both)
        lax.fori_loop(1, PROMPTS, lambda o, c: (rs_copy(o).start(), c)[1], 0)

    def stage_gather():
        lax.fori_loop(1, PROMPTS, lambda o, c: (rs_copy(o).wait(), c)[1], 0)
        total = comb[zed]
        for o in range(1, PROMPTS):
            total = total + decode(rs_recv[o, 0:HALF], rs_recv[o, HALF : HALF + TAIL])
        ag[core, zed] = encode(total)
        lax.fori_loop(1, PROMPTS, lambda o, c: (ag_copy(o).start(), c)[1], 0)
        hand_copy(0).start()

    def stage_hand():
        def forward(o, c):
            ag_copy(o).wait()
            hand_copy(o).start()
            return c

        lax.fori_loop(1, PROMPTS, forward, 0)

    steps = HEADS // HB
    stages = ((STAGE_SUM, stage_sum), (STAGE_SCATTER, stage_scatter), (STAGE_GATHER, stage_gather), (STAGE_HAND, stage_hand))

    def loop_b(i, c):
        for at, stage in stages:
            if at < steps:
                pl.when(i == at)(stage)
        phase_b([i * HB + n for n in range(HB)])
        return c

    lax.fori_loop(0, steps, loop_b, 0)
    gb_ref[0] = gb_s[...].T[:HEADS].astype(BF16)
    for at, stage in stages:
        if at >= steps:
            stage()
    lax.fori_loop(0, PROMPTS, lambda o, c: (hand_copy(o).wait(), c)[1], 0)
    for p in range(PROMPTS):
        for c in range(2):
            gf_ref[p, 0, HALF * c : HALF * c + HALF] = decode(ag[c, p, 0:HALF], ag[c, p, HALF : HALF + TAIL])


def hand_out(*refs):
    count = (len(refs) - 2) // 3
    ins, outs, bufs = refs[:count], refs[count : 2 * count], refs[2 * count : 3 * count]
    in_sem, out_sem = refs[-2:]

    def load(n):
        return pltpu.make_async_copy(ins[n], bufs[n], in_sem.at[n])

    def save(n):
        return pltpu.make_async_copy(bufs[n], outs[n], out_sem.at[n])

    for n in range(count):
        load(n).start()
    for n in range(count):
        load(n).wait()
        save(n).start()
    for n in range(count):
        save(n).wait()


def pass_on(arrays):
    anywhere = pl.BlockSpec(memory_space=pl.ANY)
    count = len(arrays)
    return pl.pallas_call(
        hand_out,
        out_shape=tuple(jax.ShapeDtypeStruct(a.shape, a.dtype) for a in arrays),
        in_specs=[anywhere] * count,
        out_specs=(anywhere,) * count,
        scratch_shapes=[pltpu.VMEM(a.shape, a.dtype) for a in arrays]
        + [pltpu.SemaphoreType.DMA((count,)), pltpu.SemaphoreType.DMA((count,))],
        name="hand_out",
    )(*arrays)


def per_device(query_rows, key_rows, value_rows, log_decay, beta_logit, out_grad, fork_state, branch_prompt, valid_len):
    vmem = pl.BlockSpec(memory_space=pltpu.VMEM)
    smem = pl.BlockSpec(memory_space=pltpu.SMEM)
    rows = jax.ShapeDtypeStruct(query_rows.shape, BF16)
    dma = pltpu.SemaphoreType.DMA
    pairs = pltpu.VMEM((HEADS, 2, D, D), BF16)
    message = pltpu.VMEM((HEADS, D + TAIL, D), I16)
    beta_rows = beta_logit.transpose(0, 2, 1)
    outs = pl.pallas_call(
        kernel,
        out_shape=(
            rows, rows, rows, rows,
            jax.ShapeDtypeStruct(beta_rows.shape, BF16),
            jax.ShapeDtypeStruct(fork_state.shape, F32),
        ),
        in_specs=[smem, smem] + [vmem] * 7,
        out_specs=(vmem,) * 6,
        scratch_shapes=[
            pltpu.VMEM((D, D), F32),
            message, message, message, message,
            pltpu.VMEM((2, PROMPTS, HALF, D), F32),
            pltpu.VMEM((PROMPTS, HALF, D), F32),
            pltpu.VMEM((PROMPTS, HALF, D), F32),
            pltpu.VMEM((PROMPTS, HALF + TAIL, D), I16),
            pltpu.VMEM((PROMPTS, HALF + TAIL, D), I16),
            pltpu.VMEM((2, PROMPTS, HALF + TAIL, D), I16),
            pltpu.VMEM((HEADS, 2, D, D), F32),
            pltpu.VMEM((HEADS, D, D), F32),
            pltpu.VMEM((HEADS, 2, D, D), F32),
            pltpu.VMEM((HEADS, 8, D), F32),
            pairs, pairs, pairs, pairs, pairs,
            pltpu.VMEM((7, D, D), BF16),
            pltpu.VMEM((2, D, D), BF16),
            pltpu.VMEM((D, D), F32),
            pltpu.VMEM((D, D), F32),
            pltpu.VMEM((D, D), F32),
            dma((HEADS,)), dma((HEADS,)),
            dma((HEADS,)), dma((HEADS,)),
            dma(()), dma(()),
            dma((PROMPTS,)), dma((PROMPTS,)),
            dma((PROMPTS,)), dma((PROMPTS,)),
            dma((PROMPTS,)), dma((PROMPTS,)),
        ],
        compiler_params=pltpu.CompilerParams(collective_id=0, has_side_effects=True),
        name="delta_backward",
    )(branch_prompt, valid_len, query_rows, key_rows, value_rows, log_decay, beta_rows, out_grad, fork_state)
    outs = pass_on(outs)
    return (*outs[:4], outs[4].transpose(0, 2, 1), outs[5])


def solution(mesh):
    branch = P(("grp", "head"), None, None)
    state = P(None, "head", None, None)
    return jax.shard_map(
        per_device,
        mesh=mesh,
        in_specs=(branch,) * 6 + (state, P(), P()),
        out_specs=(branch,) * 5 + (state,),
        check_vma=False,
    )
```

```python
import jax
import jax.numpy as jnp
from jax import lax
from jax.experimental import pallas as pl
from jax.experimental.pallas import tpu as pltpu
from jax.sharding import PartitionSpec as P

F32 = jnp.float32
BF16 = jnp.bfloat16
I16 = jnp.int16
MESH = pl.DeviceIdType.MESH
D = 128
HALF = 64
HEADS = 16
GROUPS = 16
PROMPTS = 8
HA = 8
HB = 4
TAIL = 16
STAGE_SUM = 1
STAGE_GATHER = 3
STAGE_HAND = 4
SCALE = D**-0.5


def dot(a, b, ca, cb):
    return lax.dot_general(a, b, (((ca,), (cb,)), ((), ())), preferred_element_type=F32)


def split(x):
    hi = x.astype(BF16)
    return hi, (x - hi.astype(F32)).astype(BF16)


def cat(parts, axis):
    return jnp.concatenate(parts, axis=axis)


def mm3(a, b, ca, cb):
    return dot(cat([a[0], a[0], a[1]], ca), cat([b[0], b[1], b[0]], cb), ca, cb)


def mm2(a, b, ca, cb):
    return dot(cat([a, a], ca), cat([b[0], b[1]], cb), ca, cb)


def encode(x):
    peak = jnp.maximum(jnp.max(jnp.abs(x), axis=0, keepdims=True), 1e-30)
    power = jnp.ceil(jnp.log2(peak))
    code = jnp.clip(jnp.round(x * jnp.exp2(15.0 - power)), -32767.0, 32767.0)
    tail = jnp.broadcast_to(power, (TAIL, x.shape[1]))
    return cat([code, tail], 0).astype(jnp.int32).astype(I16)


def decode(code, tail):
    power = tail[0:1].astype(jnp.int32).astype(F32)
    return code.astype(jnp.int32).astype(F32) * jnp.exp2(power - 15.0)


def kernel(
    prompt_ref, len_ref, q_ref, k_ref, v_ref, g_ref, beta_ref, do_ref, fork_ref,
    gq_ref, gk_ref, gv_ref, gg_ref, gb_ref, gf_ref,
    s_own, s_send, s_recv, ds_send, ds_recv, comb, rs_send, rs_recv, ag,
    u_s, w_s, decay_s, ee_s, qf_s, kf_s, ke_s, kt_s, tt_s, mask_s, tri_s, beta_s, betat_s, gb_s,
    s_ssem, s_rsem, d_ssem, d_rsem, r_ssem, r_rsem, a_ssem, a_rsem, f_ssem, f_rsem,
):
    grp = lax.axis_index("grp")
    me = lax.axis_index("head")
    core = lax.rem(grp, 2)
    zed = grp // 2
    base = grp * HEADS

    def head_peer(o):
        return (grp, lax.rem(me + o, HEADS))

    def chip_peer(o, x):
        return (zed * 2 + x, lax.rem(me + o, HEADS))

    def z_peer(o):
        return (lax.rem(zed + o, PROMPTS) * 2 + core, me)

    partner = (zed * 2 + 1 - core, me)

    barrier = pltpu.get_barrier_semaphore()

    def greet_head(o, c):
        for x in range(2):
            pl.semaphore_signal(barrier, inc=1, device_id=chip_peer(o, x), device_id_type=MESH)
        return c

    def greet_z(o, c):
        pl.semaphore_signal(barrier, inc=1, device_id=z_peer(o), device_id_type=MESH)
        return c

    lax.fori_loop(1, HEADS, greet_head, 0)
    lax.fori_loop(1, PROMPTS, greet_z, 0)
    pl.semaphore_signal(barrier, inc=1, device_id=partner, device_id_type=MESH)

    def pack_state(o, c):
        s_send[o] = encode(fork_ref[prompt_ref[base + lax.rem(me + o, HEADS)], 0])
        return c

    s_recv[0] = encode(fork_ref[prompt_ref[base + me], 0])
    s_own[...] = fork_ref[prompt_ref[base + me], 0]
    lax.fori_loop(1, HEADS, pack_state, 0)

    row = lax.broadcasted_iota(jnp.int32, (D, D), 0)
    col = lax.broadcasted_iota(jnp.int32, (D, D), 1)
    xor = jnp.where(row < col, jnp.bitwise_xor(row, col), 0)
    for level in range(7):
        m = 1 << level
        mask_s[level] = jnp.where((xor >= m) & (xor < 2 * m), 1.0, 0.0).astype(BF16)
    lower = jnp.where(col <= row, 1.0, 0.0) - jnp.where(col < HALF, 1.0, 0.0)
    tri_s[0] = lower.astype(BF16)
    tri_s[1] = jnp.where(col >= row, 1.0, 0.0).astype(BF16)
    valid = len_ref[base + me]
    keep_lane = jnp.where(lax.broadcasted_iota(jnp.int32, (1, D), 1) < valid, 1.0, 0.0)
    beta_rows = jax.nn.sigmoid(beta_ref[0].astype(F32)) * keep_lane
    beta_pad = cat([beta_rows, jnp.zeros((D - HEADS, D), F32)], 0)
    betat_s[...] = beta_pad
    beta_s[...] = beta_pad.T
    gb_s[...] = jnp.zeros((D, D), F32)

    pl.semaphore_wait(barrier, 2 * (HEADS - 1) + PROMPTS - 1 + 1)

    def state_copy(o):
        return pltpu.make_async_remote_copy(
            src_ref=s_send.at[o], dst_ref=s_recv.at[o], send_sem=s_ssem.at[o], recv_sem=s_rsem.at[o],
            device_id=head_peer(o), device_id_type=MESH)

    def send_state(o, c):
        state_copy(o).start()
        return c

    lax.fori_loop(1, HEADS, send_state, 0)

    def head_lanes(h):
        return pl.ds(pl.multiple_of(h * D, D), D)

    def beta_column(h):
        return jnp.sum(jnp.where(col == h, beta_s[...], 0.0), axis=1, keepdims=True)

    def keep_rows():
        return lax.broadcasted_iota(jnp.int32, (D, 1), 0) < valid

    def slot_of(h):
        return lax.rem(h - me + HEADS, HEADS)

    def grad_copy(h, x):
        o = slot_of(h)
        return pltpu.make_async_remote_copy(
            src_ref=ds_send.at[o, x], dst_ref=ds_recv.at[o, core], send_sem=d_ssem.at[o, x], recv_sem=d_rsem.at[o, core],
            device_id=(zed * 2 + x, h), device_id_type=MESH)

    def unit_parts(h):
        lanes = head_lanes(h)
        q = q_ref[0, :, lanes].astype(F32)
        k = k_ref[0, :, lanes].astype(F32)
        rq = lax.rsqrt(jnp.sum(q * q, axis=1, keepdims=True) + 1e-6)
        rk = lax.rsqrt(jnp.sum(k * k, axis=1, keepdims=True) + 1e-6)
        return q, k, rq, rk

    def masked_grad(h):
        return jnp.where(keep_rows(), do_ref[0, :, head_lanes(h)].astype(F32), 0.0).astype(BF16)

    def decay_rows(h):
        return jnp.where(keep_rows(), g_ref[0, :, head_lanes(h)].astype(F32), 0.0)

    def prepare(h):
        q, k, rq, rk = unit_parts(h)
        uq, uk = q * (rq * SCALE), k * rk
        decay = decay_rows(h)
        cum = dot(tri_s[0], decay.astype(BF16), 1, 0)
        ee = jnp.exp(decay[0:1] - cum[0:1])
        eg = jnp.exp(cum)
        es = jnp.exp(-cum)
        qf, kf = uq * eg, uk * eg
        qfs, kfs, kes = split(qf), split(kf), split(uk * es)
        qts, kts = split(qf * ee), split(kf * ee)
        u_s[h, 0], u_s[h, 1] = uq, uk
        decay_s[h, 0], decay_s[h, 1] = eg, es
        ee_s[h] = jnp.broadcast_to(ee, (8, D))
        for i in range(2):
            qf_s[h, i], kf_s[h, i], ke_s[h, i], kt_s[h, i] = qfs[i], kfs[i], kes[i], kts[i]
        return qfs, kfs, kes, qts, kts

    def couple(h, qfs, kfs, kes):
        both = tuple(cat([kfs[i], qfs[i]], 0) for i in range(2))
        scores = mm3(kes, both, 1, 1)
        beta_row = betat_s[pl.ds(h, 1), :]
        coupling = split(jnp.where(row < col, scores[:, :D] * beta_row, 0.0))
        attend = split(jnp.where(row <= col, scores[:, D:], 0.0))
        return coupling, attend

    def phase_a(hs):
        prep = [prepare(h) for h in hs]
        scores = [couple(h, *p[:3]) for h, p in zip(hs, prep)]
        dos = [masked_grad(h) for h in hs]
        dus = [split(dot(cat([a[0], a[1]], 1), cat([do, do], 0), 1, 0)) for (_, a), do in zip(scores, dos)]
        eye = jnp.where(row == col, 1.0, 0.0)
        invs = [eye - (c[0] * mask_s[0]).astype(F32) - (c[1] * mask_s[0]).astype(F32) for c, _ in scores]
        for level in range(1, 7):
            mask = mask_s[level]
            inv_ps = [split(x) for x in invs]
            size = 1 << level
            if size >= 16:
                spots = range(0, D, 2 * size)
                even = lambda x: cat([x[r : r + size] for r in spots], 0)
                gap = jnp.zeros((size, D), BF16)

                def spread(x):
                    return cat([y for n in range(len(spots)) for y in (x[n * size : (n + 1) * size], gap)], 0)

                masked = even(mask)
                steps_f = [
                    mm3((even(c[0]) * masked, even(c[1]) * masked), ip, 1, 0)
                    for (c, _), ip in zip(scores, inv_ps)]
                steps_p = [tuple(spread(y) for y in split(x)) for x in steps_f]
                outs = [mm3((even(ip[0]), even(ip[1])), sp, 1, 0) for ip, sp in zip(inv_ps, steps_p)]
                invs = [
                    cat([y for n, r in enumerate(spots) for y in (
                        x[r : r + size] - z[n * size : (n + 1) * size], x[r + size : r + 2 * size])], 0)
                    for x, z in zip(invs, outs)]
                continue
            steps_f = [mm3((c[0] * mask, c[1] * mask), ip, 1, 0) for (c, _), ip in zip(scores, inv_ps)]
            steps_p = [split(x) for x in steps_f]
            invs = [x - mm3(ip, sp, 1, 0) for x, ip, sp in zip(invs, inv_ps, steps_p)]
        inv_ps = [split(x) for x in invs]
        for h, ip in zip(hs, inv_ps):
            tt_s[h, 0], tt_s[h, 1] = ip
        ws = [mm3(ip, du, 1, 0) for ip, du in zip(inv_ps, dus)]
        nbws = []
        for h, w in zip(hs, ws):
            w_s[h] = w
            nbws.append(split(-(beta_column(h) * w)))
        dss = [
            dot(
                cat([p[3][0], p[3][1], p[4][0], p[4][0], p[4][1]], 0),
                cat([do, do, nbw[0], nbw[1], nbw[0]], 0), 0, 0)
            for p, do, nbw in zip(prep, dos, nbws)]
        for h, ds in zip(hs, dss):
            for x in range(2):
                ds_send[slot_of(h), x] = encode(ds[HALF * x : HALF * x + HALF])

    def phase_b(hs):
        pair = lambda ref: [(ref[h, 0], ref[h, 1]) for h in hs]
        betas = [beta_column(h) for h in hs]
        kts, tts = pair(kt_s), pair(tt_s)
        sss = []
        for h in hs:
            o = lax.rem(me - h + HEADS, HEADS)
            state = decode(s_recv[o, 0:D], s_recv[o, D : D + TAIL])
            sss.append(split(jnp.where(o == 0, s_own[...], state)))
        reads = [mm3(kt, ss, 1, 0) for kt, ss in zip(kts, sss)]
        targets = [
            split(b * (v_ref[0, :, head_lanes(h)].astype(F32) - r))
            for h, b, r in zip(hs, betas, reads)]
        us = [mm3(tt, tg, 0, 0) for tt, tg in zip(tts, targets)]
        usp = [split(u) for u in us]
        dos = [masked_grad(h) for h in hs]
        nbw_fs = [-(b * w_s[h]) for h, b in zip(hs, betas)]
        nbws = [split(x) for x in nbw_fs]
        dps = [split(jnp.where(row >= col, mm2(do, u, 1, 1), 0.0)) for do, u in zip(dos, usp)]
        dns = [split(jnp.where(row > col, mm3(nbw, u, 1, 1), 0.0)) for nbw, u in zip(nbws, usp)]
        kes, kfs, qfs = pair(ke_s), pair(kf_s), pair(qf_s)
        ees = [ee_s[h][0:1] for h in hs]
        dqfs = [mm2(do, ss, 1, 1) * ee + mm3(dp, ke, 1, 0) for do, ss, ee, dp, ke in zip(dos, sss, ees, dps, kes)]
        dkfs = [mm3(nbw, ss, 1, 1) * ee + mm3(dn, ke, 1, 0) for nbw, ss, ee, dn, ke in zip(nbws, sss, ees, dns, kes)]
        dkes = [
            dot(
                cat([dn[0], dn[0], dn[1], dp[0], dp[0], dp[1]], 0),
                cat([kf[0], kf[1], kf[0], qf[0], qf[1], qf[0]], 0), 0, 0)
            for dn, dp, kf, qf in zip(dns, dps, kfs, qfs)]
        for n, h in enumerate(hs):
            lanes = head_lanes(h)
            keep = keep_rows()
            uq, uk = u_s[h, 0], u_s[h, 1]
            eg, es = decay_s[h, 0], decay_s[h, 1]
            dqg, dkg, dks = dqfs[n] * eg, dkfs[n] * eg, dkes[n] * es
            dc = split(dqg * uq + dkg * uk - dks * uk)
            dg = mm2(tri_s[1], dc, 1, 0)
            gg_ref[0, :, lanes] = jnp.where(keep, dg, 0.0).astype(BF16)
            _, _, rq, rk = unit_parts(h)
            duk = dkg + dks
            gq = rq * (SCALE * dqg - uq * (jnp.sum(uq * dqg, axis=1, keepdims=True) * (1.0 / SCALE)))
            gk = rk * (duk - uk * jnp.sum(uk * duk, axis=1, keepdims=True))
            gq_ref[0, :, lanes] = gq.astype(BF16)
            gk_ref[0, :, lanes] = gk.astype(BF16)
            gv_ref[0, :, lanes] = (-nbw_fs[n]).astype(BF16)
            db = jnp.where(keep, (1.0 - betas[n]) * jnp.sum(w_s[h] * us[n], axis=1, keepdims=True), 0.0)
            gb_s[...] = jnp.where(col == h, db, gb_s[...])

    def loop_a(i, c):
        first = lax.rem(me // HA + i + 1, HEADS // HA) * HA
        phase_a([first + n for n in range(HA)])
        for n in range(HA):
            h = first + n

            for x in range(2):

                @pl.when((h != me) | (core != x))
                def _():
                    grad_copy(h, x).start()

        return c

    lax.fori_loop(0, HEADS // HA, loop_a, 0)

    def wait_state(o, c):
        state_copy(o).wait()
        return c

    lax.fori_loop(1, HEADS, wait_state, 0)

    def rs_copy(o):
        return pltpu.make_async_remote_copy(
            src_ref=rs_send.at[lax.rem(zed + o, PROMPTS)], dst_ref=rs_recv.at[o],
            send_sem=r_ssem.at[o], recv_sem=r_rsem.at[o], device_id=z_peer(o), device_id_type=MESH)

    def piece(p, c):
        return ag.at[c, p]

    def ag_copy(o):
        return pltpu.make_async_remote_copy(
            src_ref=piece(zed, core), dst_ref=piece(zed, core),
            send_sem=a_ssem.at[o], recv_sem=a_rsem.at[o], device_id=z_peer(o), device_id_type=MESH)

    def hand_copy(o):
        p = lax.rem(zed - o + PROMPTS, PROMPTS)
        return pltpu.make_async_remote_copy(
            src_ref=piece(p, core), dst_ref=piece(p, core),
            send_sem=f_ssem.at[o], recv_sem=f_rsem.at[o], device_id=partner, device_id_type=MESH)

    def stage_sum():
        def wait_grad(o, c):
            for x in range(2):

                @pl.when((o != 0) | (core != x))
                def _():
                    pltpu.make_async_remote_copy(
                        src_ref=ds_send.at[o, x], dst_ref=ds_recv.at[o, x], send_sem=d_ssem.at[o, x],
                        recv_sem=d_rsem.at[o, x], device_id=chip_peer(o, x), device_id_type=MESH).wait()

            return c

        lax.fori_loop(0, HEADS, wait_grad, 0)
        ds_recv[0, core] = ds_send[0, core]
        wide = 2 * HEADS * 8
        r64 = lax.broadcasted_iota(jnp.int32, (HALF, wide), 0)
        c64 = lax.broadcasted_iota(jnp.int32, (HALF, wide), 1)
        source = jnp.zeros((HALF, wide), jnp.int32)
        for n in range(2 * HEADS):
            branch = (zed * 2 + n % 2) * HEADS + lax.rem(me - n // 2 + HEADS, HEADS)
            source = jnp.where(c64 // 8 == n, prompt_ref[branch], source)
        hit = (source == r64 // 8) & (lax.rem(c64, 8) == lax.rem(r64, 8))
        pick = jnp.where(hit, 1.0, 0.0).astype(BF16)
        pick = cat([pick, pick], 1)

        def sum_rows(r, c):
            rows = pl.ds(pl.multiple_of(r * 16, 16), 16)
            parts = [
                decode(ds_recv[n // 2, n % 2, rows, :], ds_recv[n // 2, n % 2, HALF : HALF + TAIL, :])
                for n in range(2 * HEADS)]
            for n in range(2):
                stack = split(cat([p[8 * n : 8 * n + 8] for p in parts], 0))
                total = dot(pick, cat(stack, 0), 1, 0)
                out_rows = pl.ds(pl.multiple_of(r * 16 + 8 * n, 8), 8)
                for p in range(PROMPTS):
                    comb[p, out_rows, :] = total[8 * p : 8 * p + 8]
            return c

        lax.fori_loop(0, HALF // 16, sum_rows, 0)
        for p in range(PROMPTS):
            rs_send[p] = encode(comb[p])
        lax.fori_loop(1, PROMPTS, lambda o, c: (rs_copy(o).start(), c)[1], 0)

    def stage_gather():
        lax.fori_loop(1, PROMPTS, lambda o, c: (rs_copy(o).wait(), c)[1], 0)
        total = comb[zed]
        for o in range(1, PROMPTS):
            total = total + decode(rs_recv[o, 0:HALF], rs_recv[o, HALF : HALF + TAIL])
        ag[core, zed] = encode(total)
        lax.fori_loop(1, PROMPTS, lambda o, c: (ag_copy(o).start(), c)[1], 0)
        hand_copy(0).start()

    def stage_hand():
        def forward(o, c):
            ag_copy(o).wait()
            hand_copy(o).start()
            return c

        lax.fori_loop(1, PROMPTS, forward, 0)

    steps = HEADS // HB
    stages = ((STAGE_SUM, stage_sum), (STAGE_GATHER, stage_gather), (STAGE_HAND, stage_hand))

    def loop_b(i, c):
        for at, stage in stages:
            if at < steps:
                pl.when(i == at)(stage)
        phase_b([i * HB + n for n in range(HB)])
        return c

    lax.fori_loop(0, steps, loop_b, 0)
    gb_ref[0] = gb_s[...].T[:HEADS].astype(BF16)
    for at, stage in stages:
        if at >= steps:
            stage()
    lax.fori_loop(0, PROMPTS, lambda o, c: (hand_copy(o).wait(), c)[1], 0)
    for p in range(PROMPTS):
        for c in range(2):
            gf_ref[p, 0, HALF * c : HALF * c + HALF] = decode(ag[c, p, 0:HALF], ag[c, p, HALF : HALF + TAIL])


def hand_out(*refs):
    count = (len(refs) - 2) // 3
    ins, outs, bufs = refs[:count], refs[count : 2 * count], refs[2 * count : 3 * count]
    in_sem, out_sem = refs[-2:]

    def load(n):
        return pltpu.make_async_copy(ins[n], bufs[n], in_sem.at[n])

    def save(n):
        return pltpu.make_async_copy(bufs[n], outs[n], out_sem.at[n])

    for n in range(count):
        load(n).start()
    for n in range(count):
        load(n).wait()
        save(n).start()
    for n in range(count):
        save(n).wait()


def pass_on(arrays):
    anywhere = pl.BlockSpec(memory_space=pl.ANY)
    count = len(arrays)
    return pl.pallas_call(
        hand_out,
        out_shape=tuple(jax.ShapeDtypeStruct(a.shape, a.dtype) for a in arrays),
        in_specs=[anywhere] * count,
        out_specs=(anywhere,) * count,
        scratch_shapes=[pltpu.VMEM(a.shape, a.dtype) for a in arrays]
        + [pltpu.SemaphoreType.DMA((count,)), pltpu.SemaphoreType.DMA((count,))],
        name="hand_out",
    )(*arrays)


def per_device(query_rows, key_rows, value_rows, log_decay, beta_logit, out_grad, fork_state, branch_prompt, valid_len):
    vmem = pl.BlockSpec(memory_space=pltpu.VMEM)
    smem = pl.BlockSpec(memory_space=pltpu.SMEM)
    rows = jax.ShapeDtypeStruct(query_rows.shape, BF16)
    dma = pltpu.SemaphoreType.DMA
    pairs = pltpu.VMEM((HEADS, 2, D, D), BF16)
    message = pltpu.VMEM((HEADS, D + TAIL, D), I16)
    halves = pltpu.VMEM((HEADS, 2, HALF + TAIL, D), I16)
    beta_rows = beta_logit.transpose(0, 2, 1)
    outs = pl.pallas_call(
        kernel,
        out_shape=(
            rows, rows, rows, rows,
            jax.ShapeDtypeStruct(beta_rows.shape, BF16),
            jax.ShapeDtypeStruct(fork_state.shape, F32),
        ),
        in_specs=[smem, smem] + [vmem] * 7,
        out_specs=(vmem,) * 6,
        scratch_shapes=[
            pltpu.VMEM((D, D), F32),
            message, message, halves, halves,
            pltpu.VMEM((PROMPTS, HALF, D), F32),
            pltpu.VMEM((PROMPTS, HALF + TAIL, D), I16),
            pltpu.VMEM((PROMPTS, HALF + TAIL, D), I16),
            pltpu.VMEM((2, PROMPTS, HALF + TAIL, D), I16),
            pltpu.VMEM((HEADS, 2, D, D), F32),
            pltpu.VMEM((HEADS, D, D), F32),
            pltpu.VMEM((HEADS, 2, D, D), F32),
            pltpu.VMEM((HEADS, 8, D), F32),
            pairs, pairs, pairs, pairs, pairs,
            pltpu.VMEM((7, D, D), BF16),
            pltpu.VMEM((2, D, D), BF16),
            pltpu.VMEM((D, D), F32),
            pltpu.VMEM((D, D), F32),
            pltpu.VMEM((D, D), F32),
            dma((HEADS,)), dma((HEADS,)),
            dma((HEADS, 2)), dma((HEADS, 2)),
            dma((PROMPTS,)), dma((PROMPTS,)),
            dma((PROMPTS,)), dma((PROMPTS,)),
            dma((PROMPTS,)), dma((PROMPTS,)),
        ],
        compiler_params=pltpu.CompilerParams(collective_id=0, has_side_effects=True),
        name="delta_backward",
    )(branch_prompt, valid_len, query_rows, key_rows, value_rows, log_decay, beta_rows, out_grad, fork_state)
    outs = pass_on(outs)
    return (*outs[:4], outs[4].transpose(0, 2, 1), outs[5])


def solution(mesh):
    branch = P(("grp", "head"), None, None)
    state = P(None, "head", None, None)
    return jax.shard_map(
        per_device,
        mesh=mesh,
        in_specs=(branch,) * 6 + (state, P(), P()),
        out_specs=(branch,) * 5 + (state,),
        check_vma=False,
    )
```
